32 devices in a mesh: member: 2 (over y), band: 4 (over z), fld: 2 (over x), sub: 2 (over core).
Axes of the slice: x: 2, y: 2, z: 4, core: 2. Of those that a mesh axis runs over, the one named last changes fastest.
Arguments:
- spectra: bfloat16 [8, 16, 3, 2, 1280], P(('member', 'band'), ('fld', 'sub')), parts along dimension 0, may hold values from -2 to 2
- legendre: bfloat16 [4, 1280, 1280], P('band'), may hold values from -0.15625 to 0.15625
- assignment: int32 [4], replicated, may hold values from 0 to 3, each once
- circle_longitudes: int32 [1280], replicated, may hold values from 12 to 5136, as said below
- coriolis: float32 [2, 1280], replicated, may hold values from -1.5 to 1.5
- weights: float32 [2, 1280], replicated, may hold values from 13 to 138
- thickness: float32 [16], P(('fld', 'sub')), may hold values from 0.5 to 5
Outputs:
- tendencies: bfloat16 [8, 16, 3, 2, 1280], P(('member', 'band'), ('fld', 'sub')), parts along dimension 0
The draws below stay inside these ranges and needn't reach their ends.
There are 2 independent parts, one for each index of `member`. The reference program is written for one: setup_inputs(seed, part) draws one part's arguments, and reference() takes and returns one part's arrays. A program takes and returns all parts, laid end to end along the dimension named above; an argument that names none is the same for every part. Nothing has to cross between parts.
Inputs may be any that keep to these rules, and one draw needn't show every extreme that they name: Each value once: slot s holds the wavenumber 320 * assignment[s]. `circle_longitudes`: row h of each hemisphere (h counted from the pole) holds between 12 + 4 h and 20 + 4 h points, a multiple of four, the same in both hemispheres; row 1279 holds 5136.
All inputs are finite; a program needn't handle non-finite values.
Results may differ from the reference program's by a relative error of at most 0.0059.
Values may be sent and summed in bfloat16 or wider, within the bound.
A program may use at most 128 MiB of HBM per device.

```python
import math
import jax
import jax.numpy as jnp

TRUNCATION = 1279
COEFFS = 1280
LAT_HALF = 1280
WAVES = 4
STRIDE = 320
LEVELS = 16


def draw_circle_longitudes(key, part):
    row_index = jnp.arange(LAT_HALF, dtype=jnp.int32)
    shortfall = jax.random.randint(key, (LAT_HALF,), 0, 3, dtype=jnp.int32)
    shortfall = jnp.where(row_index == LAT_HALF - 1, 0, shortfall)
    return (20 + 4 * row_index - 4 * shortfall).astype(jnp.int32)


def block_levels(key, dims, split, least, largest):
    gain = 1.0
    for position, shards_of in split:
        steps = jax.random.uniform(jax.random.fold_in(jax.random.fold_in(key, 6), position), (shards_of,), jnp.float32, least / len(split), largest / len(split))
        gain = gain * jnp.repeat(jnp.exp(steps), dims[position] // shards_of).reshape((-1,) + (1,) * (len(dims) - 1 - position))
    return gain


def normal_values(key, shape, scale, limit, cuts=(), kind=jnp.bfloat16):
    values = scale * jax.random.normal(key, shape, jnp.float32)
    if cuts:
        values = values * block_levels(key, shape, cuts, -0.22, 0.18)
    return jnp.clip(values, -limit, limit).astype(kind)


def setup_inputs(seed: int = 0, part: int = 0) -> dict:
    splits = jax.random.split(jax.random.key(seed), 8)
    own_keys = jax.random.split(jax.random.fold_in(splits[7], part), 8)
    return {
        "spectra": normal_values(own_keys[0], (WAVES, LEVELS, 3, 2, COEFFS), 0.15, 2.0, ((0, 4), (1, 4))),
        "legendre": normal_values(splits[1], (WAVES, COEFFS, LAT_HALF), COEFFS ** -0.5, 0.15625, ((0, 4),)),
        "assignment": jax.random.permutation(splits[2], WAVES).astype(jnp.int32),
        "circle_longitudes": draw_circle_longitudes(jax.random.fold_in(splits[7], 71), part),
        "coriolis": jnp.clip(jax.random.uniform(splits[4], (2, LAT_HALF), jnp.float32, -1.5, 1.5), -1.5, 1.5),
        "weights": jnp.clip(jnp.exp(jax.random.uniform(splits[5], (2, LAT_HALF), jnp.float32, math.log(13.0), math.log(138.0))), 13.0, 138.0),
        "thickness": jnp.clip(jnp.exp(math.log(5.0) - 2.3025851 * jax.random.uniform(splits[6], (LEVELS,), jnp.float32) ** block_levels(splits[6], (LEVELS,), ((0, 4),), -0.2, 0.2)), 0.5, 5.0),
    }


TWO_PI = 6.283185307179586


def wave_masks(wavenumbers, coeff_count):
    row_index = jnp.arange(coeff_count, dtype=jnp.int32)
    inside = row_index[None, :] < (coeff_count - wavenumbers)[:, None]
    part_index = jnp.arange(2, dtype=jnp.int32)
    real_ok = (part_index[None, :] == 0) | (wavenumbers[:, None] > 0)
    return inside[:, None, :] & real_ok[:, :, None]


def trig_tables(wavenumbers, counts, row_bound):
    positions = jnp.arange(row_bound, dtype=jnp.int32)
    phase_index = (wavenumbers[None, :, None] * positions[None, None, :]) % counts[:, None, None]
    angles = TWO_PI * phase_index.astype(jnp.float32) / counts[:, None, None].astype(jnp.float32)
    inside_row = positions[None, None, :] < counts[:, None, None]
    cosine = jnp.where(inside_row, jnp.cos(angles), 0.0)
    sine_part = jnp.where(inside_row, jnp.sin(angles), 0.0)
    return jnp.stack([cosine, sine_part], axis=1).astype(jnp.bfloat16)


def inverse_factor(wavenumbers, counts):
    resolved = 2 * wavenumbers[None, :] < counts[:, None]
    gain_value = jnp.where(resolved, jnp.where(wavenumbers[None, :] == 0, 1.0, 2.0), 0.0)
    sign_pair = jnp.array([1.0, -1.0], dtype=jnp.float32)
    return gain_value[:, None, :] * sign_pair[None, :, None]


def direct_scale(wavenumbers, counts, quadrature):
    resolved = 2 * wavenumbers[None, :] < counts[:, None]
    unit_multiplier = jnp.where(resolved, 1.0, 0.0) / counts[:, None].astype(jnp.float32)
    sign_pair = jnp.array([1.0, -1.0], dtype=jnp.float32)
    return quadrature[:, :, None, None] * sign_pair[None, None, :, None] * unit_multiplier[:, None, None, :]


def tendency_terms(physical_samples, planetary):
    vorticity = physical_samples[:, :, :, 0]
    spreading_rate_grid = physical_samples[:, :, :, 1]
    thermal_state = physical_samples[:, :, :, 2]
    absolute = vorticity + planetary[:, :, None, None]
    return jnp.stack([-absolute * spreading_rate_grid, absolute * vorticity,
                      0.5 * (vorticity * vorticity + spreading_rate_grid * spreading_rate_grid),
                      -thermal_state * spreading_rate_grid], axis=3).astype(jnp.bfloat16)


def reference(spectra, legendre, assignment, circle_longitudes, coriolis, weights, thickness):
    wavenumbers = (STRIDE * assignment).astype(jnp.int32)
    keeper = wave_masks(wavenumbers, COEFFS)
    masked = jnp.where(keeper[:, None, None, :, :], spectra, jnp.zeros_like(spectra))
    parity = jnp.where(jnp.arange(COEFFS) % 2 == 0, 1.0, -1.0).astype(jnp.float32)
    legendre_wide = legendre.astype(jnp.float32)
    masked_wide = masked.astype(jnp.float32)
    north_part = jnp.einsum('ktp,klfrt->klfrp', legendre_wide, masked_wide)
    austral_portion = jnp.einsum('ktp,klfrt->klfrp', legendre_wide, masked_wide * parity)
    fourier = jnp.stack([north_part, austral_portion], axis=1).astype(jnp.bfloat16)
    group_rows = min(32, LAT_HALF)
    back_parts = []
    for group_offset in range(0, LAT_HALF, group_rows):
        group_end = group_offset + group_rows
        row_bound = 20 + 4 * (group_end - 1)
        row_bound = -(-row_bound // 128) * 128
        counts = circle_longitudes[group_offset:group_end]
        tables = trig_tables(wavenumbers, counts, row_bound)
        gain_lookup = jnp.transpose(inverse_factor(wavenumbers, counts), (2, 1, 0)).astype(jnp.bfloat16)
        coeff_block = fourier[..., group_offset:group_end] * gain_lookup[:, None, None, None, :, :]
        physical_samples = jnp.einsum('kelfrj,jrkx->jelfx', coeff_block.astype(jnp.float32), tables.astype(jnp.float32))
        planetary = jnp.transpose(coriolis[:, group_offset:group_end])
        tendency = tendency_terms(physical_samples, planetary)
        summed = jnp.einsum('jelqx,jrkx->kelqrj', tendency.astype(jnp.float32), tables.astype(jnp.float32))
        quadrature = jnp.transpose(weights[:, group_offset:group_end])
        factor = jnp.transpose(direct_scale(wavenumbers, counts, quadrature), (3, 1, 2, 0))
        back_parts.append((summed * factor[:, :, None, None, :, :]).astype(jnp.bfloat16))
    returned = jnp.concatenate(back_parts, axis=5)
    projected = jnp.einsum('ktp,kelqrp->kelqrt', legendre_wide, returned.astype(jnp.float32))
    combined = projected[:, 0] + parity * projected[:, 1]
    weighted = masked[:, :, 2].astype(jnp.float32) * thickness[None, :, None, None]
    column = jnp.cumsum(weighted[:, ::-1], axis=1)[:, ::-1]
    degree = wavenumbers[:, None] + jnp.arange(COEFFS, dtype=jnp.int32)[None, :]
    laplace = (degree * (degree + 1)).astype(jnp.float32) / float(TRUNCATION * (TRUNCATION + 1))
    divergence_tend = combined[:, :, 1] + laplace[:, None, None, :] * (column + combined[:, :, 2])
    result = jnp.stack([combined[:, :, 0], divergence_tend, combined[:, :, 3]], axis=2)
    result = jnp.where(keeper[:, None, None, :, :], result, 0.0)
    return result.astype(jnp.bfloat16)
```

```python
import jax
import jax.numpy as jnp
from jax import lax
from jax.sharding import PartitionSpec as P

TWO_PI = 6.283185307179586


def on_device(spectra, legendre, assignment, circle_longitudes, coriolis, weights, thickness):
    levels = spectra.shape[1]
    coeff_count = spectra.shape[4]
    lat_half = legendre.shape[2]
    band_count = lax.axis_size("band")
    band_place = lax.axis_index("band")
    wave_total = spectra.shape[0] * band_count
    stride = coeff_count // wave_total
    slots = lat_half // band_count
    pairs = 2 * levels
    own_wave = stride * lax.dynamic_slice_in_dim(assignment, band_place, 1)[0]
    index = jnp.arange(coeff_count, dtype=jnp.int32)
    parity = jnp.where(index % 2 == 0, 1.0, -1.0).astype(jnp.float32)
    inside = index < coeff_count - own_wave
    real_ok = (jnp.arange(2) == 0) | (own_wave > 0)
    keeper = inside[None, :] & real_ok[:, None]
    masked = jnp.where(keeper, spectra[0], jnp.zeros_like(spectra[0]))
    ordered = jnp.transpose(masked, (1, 2, 0, 3))
    stacked = jnp.stack([ordered, ordered * parity.astype(jnp.bfloat16)], axis=2)
    stacked = stacked.reshape(6 * pairs, coeff_count)
    fourier = jnp.dot(stacked, legendre[0], preferred_element_type=jnp.float32)
    fourier = fourier.astype(jnp.bfloat16)
    outgoing = jnp.transpose(fourier.reshape(6 * pairs, band_count, slots), (1, 0, 2))
    arrived = lax.all_to_all(outgoing, "band", split_axis=0, concat_axis=0, tiled=True)

    first = band_place * slots
    counts = lax.dynamic_slice_in_dim(circle_longitudes, first, slots)
    planet = lax.dynamic_slice_in_dim(coriolis, first, slots, axis=1)
    quad = lax.dynamic_slice_in_dim(weights, first, slots, axis=1)
    most = 3 * (wave_total - 1) + 1
    ratio = counts // stride
    aliased = (ratio * stride == counts) & (ratio < most)
    points = jnp.where(aliased, ratio, most)
    xs = jnp.arange(most, dtype=jnp.int32)
    phase = (assignment[:, None, None] * xs[None, :, None]) % points[None, None, :]
    angles = TWO_PI * phase.astype(jnp.float32) / points.astype(jnp.float32)
    live = xs[None, :, None] < points[None, None, :]
    tables = jnp.stack(
        [jnp.where(live, jnp.cos(angles), 0.0), jnp.where(live, -jnp.sin(angles), 0.0)], axis=1
    )
    waves = stride * assignment
    resolved = 2 * waves[:, None] < counts[None, :]
    gain = jnp.where(resolved, jnp.where(waves[:, None] == 0, 1.0, 2.0), 0.0)
    coeffs = arrived.astype(jnp.float32).reshape(wave_total, 3, 2, pairs, slots)
    coeffs = coeffs * gain[:, None, None, None, :]
    grid = jnp.sum(
        coeffs[:, :, :, None] * tables[:, None, :, :, None, :], axis=(0, 2)
    )
    vort, div, theta = grid[0], grid[1], grid[2]
    spin = jnp.broadcast_to(planet[:, None, :], (2, levels, slots)).reshape(pairs, slots)
    absolute = vort + spin
    terms = jnp.stack(
        [-absolute * div, absolute * vort, 0.5 * (vort * vort + div * div), -theta * div]
    )
    summed = jnp.sum(
        terms[None, :, None] * tables[:, None, :, :, None, :], axis=3
    )
    quad = jnp.broadcast_to(quad[:, None, :], (2, levels, slots)).reshape(pairs, slots)
    scale = jnp.where(resolved, 1.0 / points.astype(jnp.float32), 0.0)[:, None, :] * quad
    returned = (summed * scale[:, None, None]).astype(jnp.bfloat16)
    returned = returned.reshape(wave_total, 8 * pairs, slots)
    landed = lax.all_to_all(returned, "band", split_axis=0, concat_axis=0, tiled=True)
    landed = jnp.transpose(landed, (1, 0, 2)).reshape(8 * pairs, lat_half)
    projected = lax.dot_general(
        landed, legendre[0], (((1,), (1,)), ((), ())), preferred_element_type=jnp.float32
    ).reshape(4, 2, 2, levels, coeff_count)
    combined = projected[:, :, 0] + parity * projected[:, :, 1]

    weighted = ordered[2].astype(jnp.float32) * thickness[None, :, None]
    partial = [weighted[:, levels - 1]]
    for level in range(levels - 2, -1, -1):
        partial.insert(0, partial[0] + weighted[:, level])
    group = lax.axis_size(("fld", "sub"))
    sums = lax.all_gather(partial[0], ("fld", "sub"))
    later = jnp.arange(group) > lax.axis_index(("fld", "sub"))
    below = jnp.sum(jnp.where(later[:, None, None], sums, 0.0), axis=0)
    column = jnp.stack(partial, axis=1) + below[:, None]
    degree = own_wave + index
    truncation = coeff_count - 1
    laplace = (degree * (degree + 1)).astype(jnp.float32) / float(truncation * (truncation + 1))
    divergence = combined[1] + laplace * (column + combined[2])
    result = jnp.stack([combined[0], divergence, combined[3]])
    result = jnp.where(keeper[None, :, None, :], result, 0.0).astype(jnp.bfloat16)
    return jnp.transpose(result, (2, 0, 1, 3))[None]


def solution(mesh):
    in_specs = (
        P(("member", "band"), ("fld", "sub"), None, None, None),
        P("band", None, None),
        P(),
        P(),
        P(),
        P(),
        P(("fld", "sub")),
    )
    out_specs = P(("member", "band"), ("fld", "sub"), None, None, None)
    return jax.shard_map(
        on_device, mesh=mesh, in_specs=in_specs, out_specs=out_specs, check_vma=False
    )
```

```python
import functools

import jax
import jax.numpy as jnp
from jax import lax
from jax.experimental import pallas as pl
from jax.experimental.pallas import tpu as pltpu
from jax.sharding import PartitionSpec as P

MESH = pl.DeviceIdType.MESH
COS_TERMS = (1.0, -1 / 2, 1 / 24, -1 / 720, 1 / 40320, -1 / 3628800, 1 / 479001600)
SIN_TERMS = (1.0, -1 / 6, 1 / 120, -1 / 5040, 1 / 362880, -1 / 39916800, 1 / 6227020800)
PI = 3.141592653589793


def each(count, body):
    if count <= 8:
        for i in range(count):
            body(i)
    else:

        def step(i, carry):
            body(i)
            return carry

        lax.fori_loop(0, count, step, 0)


def series(terms, square):
    value = jnp.full_like(square, terms[-1])
    for term in terms[-2::-1]:
        value = value * square + term
    return value


def circle(turns):
    half = PI * turns
    square = half * half
    sine = half * series(SIN_TERMS, square)
    cosine = series(COS_TERMS, square)
    return 1.0 - 2.0 * sine * sine, 2.0 * sine * cosine


def kernel(
    sizes, spectra, legendre, assignment, thickness, rows, out,
    table, wide, fsend, frecv, costab, sintab, coeffs, sums, bsend, brecv, proj,
    local, colsend, colrecv, load_sem, fs_sem, fr_sem, bs_sem, br_sem, cs_sem, cr_sem,
):
    band, group, subs, stride, levels, coeff, lat, block, most = sizes
    pairs = 2 * levels
    me = lax.axis_index("band")
    mine = lax.axis_index("fld") * subs + lax.axis_index("sub")

    def band_peer(k):
        return {"band": lax.rem(me + k, band)}

    def group_peer(k):
        peer = lax.rem(mine + k, group)
        return {"fld": peer // subs, "sub": lax.rem(peer, subs)}

    load = pltpu.make_async_copy(legendre.at[0], table.at[:, pl.ds(0, lat)], load_sem)
    load.start()
    barrier = pltpu.get_barrier_semaphore()

    def greet_band(k):
        pl.semaphore_signal(barrier, inc=1, device_id=band_peer(k + 1), device_id_type=MESH)

    def greet_group(k):
        pl.semaphore_signal(barrier, inc=1, device_id=group_peer(k + 1), device_id_type=MESH)

    each(band - 1, greet_band)
    each(group - 1, greet_group)

    own = stride * assignment[me]
    index = lax.broadcasted_iota(jnp.int32, (2, coeff), 1)
    part = lax.broadcasted_iota(jnp.int32, (2, coeff), 0)
    keep = (index < coeff - own) & (part * jnp.where(own == 0, 1, 0) == 0)
    parity = (1 - 2 * lax.rem(index, 2)).astype(jnp.float32)
    for level in range(levels):
        for field in range(3):
            value = jnp.where(keep, spectra[0, level, field].astype(jnp.float32), 0.0)
            other = value * parity
            for r in range(2):
                row = (2 * field + r) * pairs + level
                wide[row : row + 1, :] = value[r : r + 1]
                wide[row + levels : row + levels + 1, :] = other[r : r + 1]
    both = wide[...].astype(jnp.bfloat16)
    if block * band > lat:
        table[:, lat:] = jnp.zeros((coeff, block * band - lat), jnp.bfloat16)
    pl.semaphore_wait(barrier, band + group - 2)
    load.wait()

    def forward(k):
        return pltpu.make_async_remote_copy(
            src_ref=fsend.at[k], dst_ref=frecv.at[me], send_sem=fs_sem.at[k],
            recv_sem=fr_sem.at[k], device_id=band_peer(k + 1), device_id_type=MESH,
        )

    def back(k):
        return pltpu.make_async_remote_copy(
            src_ref=bsend.at[k], dst_ref=brecv.at[me], send_sem=bs_sem.at[k],
            recv_sem=br_sem.at[k], device_id=band_peer(k + 1), device_id_type=MESH,
        )

    def across(k):
        return pltpu.make_async_remote_copy(
            src_ref=colsend, dst_ref=colrecv.at[mine], send_sem=cs_sem.at[k],
            recv_sem=cr_sem.at[k], device_id=group_peer(k + 1), device_id_type=MESH,
        )

    def lanes(b):
        return pl.ds(pl.multiple_of(b * block, 128), block)

    def transform(b):
        return jnp.dot(both, table[:, lanes(b)], preferred_element_type=jnp.float32).astype(
            jnp.bfloat16
        )

    def send_forward(k):
        fsend[k] = transform(lax.rem(me + k + 1, band))
        forward(k).start()

    each(band - 1, send_forward)
    frecv[me] = transform(me)

    for r in range(2):
        total = None
        for level in range(levels - 1, -1, -1):
            row = (4 + r) * pairs + level
            value = thickness[level] * wide[row : row + 1, :]
            total = value if total is None else total + value
            local[r, level : level + 1, :] = total
        colsend[r : r + 1, :] = total
    each(group - 1, lambda k: across(k).start())

    points = rows[0:1, lanes(me)]
    inverse = rows[1:2, lanes(me)]
    counts = rows[2:3, lanes(me)]
    pair = lax.broadcasted_iota(jnp.int32, (pairs, block), 0)
    spin = jnp.where(pair < levels, rows[3:4, lanes(me)], rows[4:5, lanes(me)])
    quad = jnp.where(pair < levels, rows[5:6, lanes(me)], rows[6:7, lanes(me)])
    height = costab.shape[1]
    xs = lax.broadcasted_iota(jnp.int32, (height, block), 0).astype(jnp.float32)

    def fill(s):
        phase = xs * assignment[s].astype(jnp.float32)
        phase = phase - points * jnp.floor(phase * inverse)
        turns = phase * inverse
        cosine, sine = circle(turns - jnp.floor(turns + 0.5))
        costab[s] = jnp.where(xs < points, cosine, 0.0)
        sintab[s] = jnp.where(xs < points, sine, 0.0)

    each(band, fill)

    def weigh(s):
        wave = (stride * assignment[s]).astype(jnp.float32)
        gain = jnp.where(2.0 * wave < counts, jnp.where(wave == 0.0, 1.0, 2.0), 0.0)
        coeffs[s] = frecv[s].astype(jnp.float32) * gain
        sums[s] = jnp.zeros(sums.shape[1:], jnp.float32)

    each(band - 1, lambda k: forward(k).wait_recv())
    each(band, weigh)

    def sample(x, carry):
        def add_wave(s, fields):
            cosine = costab[s, pl.ds(x, 1), :]
            sine = sintab[s, pl.ds(x, 1), :]
            return tuple(
                fields[f]
                + coeffs[s, 2 * f * pairs : (2 * f + 1) * pairs, :] * cosine
                - coeffs[s, (2 * f + 1) * pairs : (2 * f + 2) * pairs, :] * sine
                for f in range(3)
            )

        fields = tuple(jnp.zeros((pairs, block), jnp.float32) for _ in range(3))
        if band <= 8:
            for s in range(band):
                fields = add_wave(s, fields)
        else:
            fields = lax.fori_loop(0, band, add_wave, fields)
        vort, div, theta = fields
        absolute = vort + spin
        terms = (
            -absolute * div,
            absolute * vort,
            0.5 * (vort * vort + div * div),
            -theta * div,
        )

        def collect(s):
            cosine = costab[s, pl.ds(x, 1), :]
            sine = sintab[s, pl.ds(x, 1), :]
            for q in range(4):
                sums[s, 2 * q * pairs : (2 * q + 1) * pairs, :] += terms[q] * cosine
                sums[s, (2 * q + 1) * pairs : (2 * q + 2) * pairs, :] -= terms[q] * sine

        each(band, collect)
        return carry

    lax.fori_loop(0, most, sample, 0)

    def finish(s):
        wave = (stride * assignment[s]).astype(jnp.float32)
        scale = jnp.where(2.0 * wave < counts, quad, 0.0)
        value = sums[s].reshape(8, pairs, block) * scale[None]
        return value.reshape(8 * pairs, block).astype(jnp.bfloat16)

    def send_back(k):
        bsend[k] = finish(lax.rem(me + k + 1, band))
        back(k).start()

    each(band - 1, send_back)
    brecv[me] = finish(me)

    def project(b):
        return lax.dot_general(
            brecv[b], table[:, lanes(b)], (((1,), (1,)), ((), ())),
            preferred_element_type=jnp.float32,
        )

    proj[...] = project(me)

    def gather_back(k):
        back(k).wait_recv()
        proj[...] += project(lax.rem(me + band - k - 1, band))

    each(band - 1, gather_back)
    each(group - 1, lambda k: across(k).wait_recv())
    below = jnp.zeros((2, coeff), jnp.float32)
    for k in range(group - 1):
        sender = lax.rem(mine + group - k - 1, group)
        below = below + jnp.where(sender > mine, 1.0, 0.0) * colrecv[sender]
    degree = own + index[0:1]
    laplace = (degree * (degree + 1)).astype(jnp.float32) * (1.0 / float((coeff - 1) * coeff))
    sign = parity[0:1]
    for r in range(2):

        def combined(q):
            value = proj[(2 * q + r) * pairs : (2 * q + r + 1) * pairs, :]
            return value[:levels] + sign * value[levels:]

        mask = jnp.where(keep, 1.0, 0.0)[r : r + 1]
        column = local[r] + below[r : r + 1]
        out[0, r] = (combined(0) * mask).astype(jnp.bfloat16)
        second = combined(1) + laplace * (column + combined(2))
        out[1, r] = (second * mask).astype(jnp.bfloat16)
        out[2, r] = (combined(3) * mask).astype(jnp.bfloat16)
    each(band - 1, lambda k: forward(k).wait_send())
    each(band - 1, lambda k: back(k).wait_send())
    each(group - 1, lambda k: across(k).wait_send())


def on_device(
    band, subs, group, spectra, legendre, assignment, circle_longitudes, coriolis, weights,
    thickness,
):
    levels, coeff, lat = spectra.shape[1], spectra.shape[4], legendre.shape[2]
    pairs = 2 * levels
    stride = coeff // band
    block = -(-lat // (128 * band)) * 128
    most = 3 * (band - 1) + 1
    height = -(-most // 8) * 8
    ratio = circle_longitudes // stride
    aliased = (ratio * stride == circle_longitudes) & (ratio < most)
    points = jnp.where(aliased, ratio, most).astype(jnp.float32)
    inverse = 1.0 / points
    rows = jnp.stack(
        [
            points, inverse, circle_longitudes.astype(jnp.float32), coriolis[0], coriolis[1],
            weights[0] * inverse, weights[1] * inverse, jnp.zeros_like(points),
        ]
    )
    rows = jnp.pad(rows, ((0, 0), (0, band * block - lat)))
    sizes = (band, group, subs, stride, levels, coeff, lat, block, most)
    vmem = pl.BlockSpec(memory_space=pltpu.VMEM)
    smem = pl.BlockSpec(memory_space=pltpu.SMEM)
    bf16, f32, dma = jnp.bfloat16, jnp.float32, pltpu.SemaphoreType.DMA
    far, near = max(band - 1, 1), max(group - 1, 1)
    result = pl.pallas_call(
        functools.partial(kernel, sizes),
        out_shape=jax.ShapeDtypeStruct((3, 2, levels, coeff), bf16),
        in_specs=[vmem, pl.BlockSpec(memory_space=pl.ANY), smem, smem, vmem],
        out_specs=vmem,
        scratch_shapes=[
            pltpu.VMEM((coeff, band * block), bf16),
            pltpu.VMEM((6 * pairs, coeff), f32),
            pltpu.VMEM((far, 6 * pairs, block), bf16),
            pltpu.VMEM((band, 6 * pairs, block), bf16),
            pltpu.VMEM((band, height, block), f32),
            pltpu.VMEM((band, height, block), f32),
            pltpu.VMEM((band, 6 * pairs, block), f32),
            pltpu.VMEM((band, 8 * pairs, block), f32),
            pltpu.VMEM((far, 8 * pairs, block), bf16),
            pltpu.VMEM((band, 8 * pairs, block), bf16),
            pltpu.VMEM((8 * pairs, coeff), f32),
            pltpu.VMEM((2, levels, coeff), f32),
            pltpu.VMEM((2, coeff), f32),
            pltpu.VMEM((group, 2, coeff), f32),
            dma,
            dma((far,)),
            dma((far,)),
            dma((far,)),
            dma((far,)),
            dma((near,)),
            dma((near,)),
        ],
        compiler_params=pltpu.CompilerParams(
            collective_id=0, has_side_effects=True, vmem_limit_bytes=48 << 20
        ),
    )(spectra, legendre, assignment, thickness, rows)
    return jnp.transpose(result, (2, 0, 1, 3))[None]


def solution(mesh):
    in_specs = (
        P(("member", "band"), ("fld", "sub"), None, None, None),
        P("band", None, None),
        P(),
        P(),
        P(),
        P(),
        P(("fld", "sub")),
    )
    out_specs = P(("member", "band"), ("fld", "sub"), None, None, None)
    subs = mesh.shape["sub"]
    part = functools.partial(on_device, mesh.shape["band"], subs, subs * mesh.shape["fld"])
    return jax.shard_map(
        part, mesh=mesh, in_specs=in_specs, out_specs=out_specs, check_vma=False
    )
```

```python
import functools

import jax
import jax.numpy as jnp
from jax import lax
from jax.experimental import pallas as pl
from jax.experimental.pallas import tpu as pltpu
from jax.sharding import PartitionSpec as P

MESH = pl.DeviceIdType.MESH
COS_TERMS = (1.0, -1 / 2, 1 / 24, -1 / 720, 1 / 40320, -1 / 3628800, 1 / 479001600)
SIN_TERMS = (1.0, -1 / 6, 1 / 120, -1 / 5040, 1 / 362880, -1 / 39916800, 1 / 6227020800)
PI = 3.141592653589793


def each(count, body):
    if count <= 8:
        for i in range(count):
            body(i)
    else:

        def step(i, carry):
            body(i)
            return carry

        lax.fori_loop(0, count, step, 0)


def series(terms, square):
    value = jnp.full_like(square, terms[-1])
    for term in terms[-2::-1]:
        value = value * square + term
    return value


def circle(turns):
    half = PI * turns
    square = half * half
    sine = half * series(SIN_TERMS, square)
    cosine = series(COS_TERMS, square)
    return 1.0 - 2.0 * sine * sine, 2.0 * sine * cosine


def kernel(
    sizes, spectra_far, legendre, assignment_far, circles_far, coriolis_far, weights_far,
    thickness_far, out, table, spectra, assignment, circles, coriolis, weights, thickness,
    wide, fsend, frecv, costab, sintab, coeffs, sums, bsend, brecv, proj, local, colsend, colrecv,
    load_sem, small_sem, fs_sem, fr_sem, bs_sem, br_sem, cs_sem, cr_sem,
):
    band, group, subs, stride, levels, coeff, lat, least, first_wide, last_wide, most = sizes
    pairs = 2 * levels
    widest = min(least + first_wide + last_wide, least + 1)
    block = 128 * widest
    me = lax.axis_index("band")
    mine = lax.axis_index("fld") * subs + lax.axis_index("sub")

    def width(b):
        wide_one = (b < first_wide) | (b >= band - last_wide)
        return jnp.where(wide_one, widest, least)

    def lanes(b):
        tile = b * least + jnp.minimum(b, first_wide) + jnp.maximum(b - (band - last_wide), 0)
        return pl.ds(pl.multiple_of(tile * 128, 128), block)

    def tiles(b, body):
        for c in range(widest):
            if c < least:
                body(c)
            else:
                pl.when(width(b) > c)(functools.partial(body, c))

    def tile(c):
        return pl.ds(128 * c, 128)

    def band_peer(k):
        return {"band": lax.rem(me + k, band)}

    def group_peer(k):
        peer = lax.rem(mine + k, group)
        return {"fld": peer // subs, "sub": lax.rem(peer, subs)}

    pairs_of = (
        (spectra_far, spectra), (assignment_far, assignment), (circles_far, circles),
        (coriolis_far, coriolis), (weights_far, weights), (thickness_far, thickness),
    )
    small = [
        pltpu.make_async_copy(far, near, small_sem.at[i]) for i, (far, near) in enumerate(pairs_of)
    ]
    load = pltpu.make_async_copy(legendre.at[0], table, load_sem)
    for copy in small:
        copy.start()
    load.start()
    if widest > least:
        frecv[:, :, 128 * least :] = jnp.zeros((band, 6 * pairs, 128), jnp.bfloat16)
        brecv[:, :, 128 * least :] = jnp.zeros((band, 8 * pairs, 128), jnp.bfloat16)
    barrier = pltpu.get_barrier_semaphore()

    def greet_band(k):
        pl.semaphore_signal(barrier, inc=1, device_id=band_peer(k + 1), device_id_type=MESH)

    def greet_group(k):
        pl.semaphore_signal(barrier, inc=1, device_id=group_peer(k + 1), device_id_type=MESH)

    each(band - 1, greet_band)
    each(group - 1, greet_group)
    for copy in small:
        copy.wait()

    own = stride * assignment[me]
    index = lax.broadcasted_iota(jnp.int32, (2, coeff), 1)
    part = lax.broadcasted_iota(jnp.int32, (2, coeff), 0)
    keep = (index < coeff - own) & (part * jnp.where(own == 0, 1, 0) == 0)
    parity = (1 - 2 * lax.rem(index, 2)).astype(jnp.float32)
    for level in range(levels):
        for field in range(3):
            value = jnp.where(keep, spectra[0, level, field].astype(jnp.float32), 0.0)
            other = value * parity
            for r in range(2):
                row = (2 * field + r) * pairs + level
                wide[row : row + 1, :] = value[r : r + 1]
                wide[row + levels : row + levels + 1, :] = other[r : r + 1]
    both = wide[...].astype(jnp.bfloat16)

    def forward(k, c):
        return pltpu.make_async_remote_copy(
            src_ref=fsend.at[k, :, tile(c)], dst_ref=frecv.at[me, :, tile(c)],
            send_sem=fs_sem.at[k, c], recv_sem=fr_sem.at[k, c], device_id=band_peer(k + 1),
            device_id_type=MESH,
        )

    def back(k, c):
        return pltpu.make_async_remote_copy(
            src_ref=bsend.at[k, :, tile(c)], dst_ref=brecv.at[me, :, tile(c)],
            send_sem=bs_sem.at[k, c], recv_sem=br_sem.at[k, c], device_id=band_peer(k + 1),
            device_id_type=MESH,
        )

    def across(k):
        return pltpu.make_async_remote_copy(
            src_ref=colsend, dst_ref=colrecv.at[mine], send_sem=cs_sem.at[k],
            recv_sem=cr_sem.at[k], device_id=group_peer(k + 1), device_id_type=MESH,
        )

    load.wait()
    pl.semaphore_wait(barrier, band + group - 2)

    def transform(b):
        return jnp.dot(both, table[:, lanes(b)], preferred_element_type=jnp.float32).astype(
            jnp.bfloat16
        )

    def send_forward(k):
        b = lax.rem(me + k + 1, band)
        fsend[k] = transform(b)
        tiles(b, lambda c: forward(k, c).start())

    each(band - 1, send_forward)
    frecv[me] = transform(me)

    for r in range(2):
        total = None
        for level in range(levels - 1, -1, -1):
            row = (4 + r) * pairs + level
            value = thickness[level] * wide[row : row + 1, :]
            total = value if total is None else total + value
            local[r, level : level + 1, :] = total
        colsend[r : r + 1, :] = total
    each(group - 1, lambda k: across(k).start())

    counts = circles[lanes(me)].astype(jnp.float32).reshape(1, block)
    ratio = jnp.floor(counts * (1.0 / stride) + 0.5)
    points = jnp.where((ratio * stride == counts) & (ratio < most), ratio, float(most))
    inverse = 1.0 / points
    height = costab.shape[2]
    xs = lax.broadcasted_iota(jnp.int32, (height, block), 0).astype(jnp.float32)
    pair = lax.broadcasted_iota(jnp.int32, (pairs, block), 0)
    lane = lax.broadcasted_iota(jnp.int32, (pairs, block), 1)
    north, south = coriolis[0:1, lanes(me)], coriolis[1:2, lanes(me)]
    spin = jnp.where(pair < levels, north, south)
    north, south = weights[0:1, lanes(me)], weights[1:2, lanes(me)]
    quad = jnp.where(pair < levels, north, south) * inverse
    quad = jnp.where(lane < 128 * width(me), quad, 0.0)

    def fill(s):
        phase = xs * assignment[s].astype(jnp.float32)
        phase = phase - points * jnp.floor(phase * inverse)
        turns = phase * inverse
        cosine, sine = circle(turns - jnp.floor(turns + 0.5))
        cosine = jnp.where(xs < points, cosine, 0.0)
        sine = jnp.where(xs < points, sine, 0.0)
        for c in range(widest):
            costab[s, c] = cosine[:, 128 * c : 128 * c + 128]
            sintab[s, c] = sine[:, 128 * c : 128 * c + 128]

    each(band, fill)

    def sample(c):
        here = slice(128 * c, 128 * c + 128)
        number = counts[:, here]

        def twice(s):
            return 2.0 * (stride * assignment[s]).astype(jnp.float32)

        def weigh(s):
            double = twice(s)
            gain = jnp.where(double < number, jnp.where(double == 0.0, 1.0, 2.0), 0.0)
            coeffs[s] = frecv[s, :, here].astype(jnp.float32) * gain

        def add_wave(x, s, fields):
            cosine = costab[s, c, pl.ds(x, 1), :]
            sine = sintab[s, c, pl.ds(x, 1), :]
            return tuple(
                fields[f]
                + coeffs[s, 2 * f * pairs : (2 * f + 1) * pairs, :] * cosine
                - coeffs[s, (2 * f + 1) * pairs : (2 * f + 2) * pairs, :] * sine
                for f in range(3)
            )

        def products(fields):
            vort, div, theta = fields
            absolute = vort + spin[:, here]
            return (
                -absolute * div,
                absolute * vort,
                0.5 * (vort * vort + div * div),
                -theta * div,
            )

        nothing = jnp.zeros((pairs, 128), jnp.float32)

        def scaled(s, q, value):
            scale = jnp.where(twice(s) < number, quad[:, here], 0.0)
            sums[s, q * pairs : (q + 1) * pairs, here] = value * scale

        each(band, weigh)
        if band <= 4:

            def point(x, totals):
                fields = (nothing,) * 3
                for s in range(band):
                    fields = add_wave(x, s, fields)
                terms = products(fields)
                result = []
                for s in range(band):
                    cosine = costab[s, c, pl.ds(x, 1), :]
                    sine = sintab[s, c, pl.ds(x, 1), :]
                    for q in range(4):
                        result.append(totals[8 * s + 2 * q] + terms[q] * cosine)
                        result.append(totals[8 * s + 2 * q + 1] - terms[q] * sine)
                return tuple(result)

            totals = lax.fori_loop(0, most, point, (nothing,) * (8 * band))
            for s in range(band):
                for q in range(8):
                    scaled(s, q, totals[8 * s + q])
        else:

            def clear(s):
                sums[s, :, here] = jnp.zeros((8 * pairs, 128), jnp.float32)

            def point(x, carry):
                fields = lax.fori_loop(
                    0, band, functools.partial(add_wave, x), (nothing,) * 3
                )
                terms = products(fields)

                def collect(s):
                    cosine = costab[s, c, pl.ds(x, 1), :]
                    sine = sintab[s, c, pl.ds(x, 1), :]
                    for q in range(4):
                        real = slice(2 * q * pairs, (2 * q + 1) * pairs)
                        imag = slice((2 * q + 1) * pairs, (2 * q + 2) * pairs)
                        sums[s, real, here] += terms[q] * cosine
                        sums[s, imag, here] -= terms[q] * sine

                each(band, collect)
                return carry

            def settle(s):
                for q in range(8):
                    scaled(s, q, sums[s, q * pairs : (q + 1) * pairs, here])

            each(band, clear)
            lax.fori_loop(0, most, point, 0)
            each(band, settle)

        def send_back(k):
            value = sums[lax.rem(me + k + 1, band), :, here]
            bsend[k, :, here] = value.astype(jnp.bfloat16)
            back(k, c).start()

        each(band - 1, send_back)
        brecv[me, :, here] = sums[me, :, here].astype(jnp.bfloat16)

    def arrive(c):
        each(band - 1, lambda k: forward(k, c).wait_recv())
        sample(c)

    tiles(me, arrive)

    def project(b):
        return lax.dot_general(
            brecv[b], table[:, lanes(b)], (((1,), (1,)), ((), ())),
            preferred_element_type=jnp.float32,
        )

    proj[...] = project(me)

    def gather_back(k):
        b = lax.rem(me + band - k - 1, band)
        tiles(b, lambda c: back(k, c).wait_recv())
        proj[...] += project(b)

    each(band - 1, gather_back)
    each(group - 1, lambda k: across(k).wait_recv())
    below = jnp.zeros((2, coeff), jnp.float32)
    for k in range(group - 1):
        sender = lax.rem(mine + group - k - 1, group)
        below = below + jnp.where(sender > mine, 1.0, 0.0) * colrecv[sender]
    degree = own + index[0:1]
    laplace = (degree * (degree + 1)).astype(jnp.float32) * (1.0 / float((coeff - 1) * coeff))
    sign = parity[0:1]
    for r in range(2):

        def combined(q):
            value = proj[(2 * q + r) * pairs : (2 * q + r + 1) * pairs, :]
            return value[:levels] + sign * value[levels:]

        mask = jnp.where(keep, 1.0, 0.0)[r : r + 1]
        column = local[r] + below[r : r + 1]
        out[0, r] = (combined(0) * mask).astype(jnp.bfloat16)
        second = combined(1) + laplace * (column + combined(2))
        out[1, r] = (second * mask).astype(jnp.bfloat16)
        out[2, r] = (combined(3) * mask).astype(jnp.bfloat16)

    def sent(k):
        tiles(lax.rem(me + k + 1, band), lambda c: forward(k, c).wait_send())
        tiles(me, lambda c: back(k, c).wait_send())

    each(band - 1, sent)
    each(group - 1, lambda k: across(k).wait_send())


def on_device(
    band, subs, group, spectra, legendre, assignment, circle_longitudes, coriolis, weights,
    thickness,
):
    levels, coeff, lat = spectra.shape[1], spectra.shape[4], legendre.shape[2]
    pairs = 2 * levels
    stride = coeff // band
    least, extra = divmod(lat // 128, band)
    last_wide = -(-extra // 2)
    block = 128 * (least + (1 if extra else 0))
    most = 3 * (band - 1) + 1
    height = -(-most // 8) * 8
    sizes = (
        band, group, subs, stride, levels, coeff, lat, least, extra - last_wide, last_wide, most,
    )
    far_away = pl.BlockSpec(memory_space=pltpu.MemorySpace.HBM)
    bf16, f32, dma = jnp.bfloat16, jnp.float32, pltpu.SemaphoreType.DMA
    far, near, many = max(band - 1, 1), max(group - 1, 1), block // 128
    result = pl.pallas_call(
        functools.partial(kernel, sizes),
        out_shape=jax.ShapeDtypeStruct((3, 2, levels, coeff), bf16),
        in_specs=[far_away] * 7,
        out_specs=pl.BlockSpec(memory_space=pltpu.VMEM),
        scratch_shapes=[
            pltpu.VMEM((coeff, lat), bf16),
            pltpu.VMEM(spectra.shape, bf16),
            pltpu.SMEM((band,), jnp.int32),
            pltpu.VMEM((lat,), jnp.int32),
            pltpu.VMEM((2, lat), f32),
            pltpu.VMEM((2, lat), f32),
            pltpu.SMEM((levels,), f32),
            pltpu.VMEM((6 * pairs, coeff), f32),
            pltpu.VMEM((far, 6 * pairs, block), bf16),
            pltpu.VMEM((band, 6 * pairs, block), bf16),
            pltpu.VMEM((band, many, height, 128), f32),
            pltpu.VMEM((band, many, height, 128), f32),
            pltpu.VMEM((band, 6 * pairs, 128), f32),
            pltpu.VMEM((band, 8 * pairs, block), f32),
            pltpu.VMEM((far, 8 * pairs, block), bf16),
            pltpu.VMEM((band, 8 * pairs, block), bf16),
            pltpu.VMEM((8 * pairs, coeff), f32),
            pltpu.VMEM((2, levels, coeff), f32),
            pltpu.VMEM((2, coeff), f32),
            pltpu.VMEM((group, 2, coeff), f32),
            dma,
            dma((6,)),
            dma((far, many)),
            dma((far, many)),
            dma((far, many)),
            dma((far, many)),
            dma((near,)),
            dma((near,)),
        ],
        compiler_params=pltpu.CompilerParams(
            collective_id=0, has_side_effects=True, vmem_limit_bytes=64 << 20
        ),
    )(
        spectra, legendre, assignment, circle_longitudes, coriolis, weights, thickness,
    )
    return jnp.transpose(result, (2, 0, 1, 3))[None]


def solution(mesh):
    in_specs = (
        P(("member", "band"), ("fld", "sub"), None, None, None),
        P("band", None, None),
        P(),
        P(),
        P(),
        P(),
        P(("fld", "sub")),
    )
    out_specs = P(("member", "band"), ("fld", "sub"), None, None, None)
    subs = mesh.shape["sub"]
    part = functools.partial(on_device, mesh.shape["band"], subs, subs * mesh.shape["fld"])
    return jax.shard_map(
        part, mesh=mesh, in_specs=in_specs, out_specs=out_specs, check_vma=False
    )
```

```python
import functools

import jax
import jax.numpy as jnp
from jax import lax
from jax.experimental import pallas as pl
from jax.experimental.pallas import tpu as pltpu
from jax.sharding import PartitionSpec as P

MESH = pl.DeviceIdType.MESH
COS_TERMS = (1.0, -1 / 2, 1 / 24, -1 / 720, 1 / 40320, -1 / 3628800, 1 / 479001600)
SIN_TERMS = (1.0, -1 / 6, 1 / 120, -1 / 5040, 1 / 362880, -1 / 39916800, 1 / 6227020800)
PI = 3.141592653589793


def each(count, body):
    if count <= 8:
        for i in range(count):
            body(i)
    else:

        def step(i, carry):
            body(i)
            return carry

        lax.fori_loop(0, count, step, 0)


def series(terms, square):
    value = jnp.full_like(square, terms[-1])
    for term in terms[-2::-1]:
        value = value * square + term
    return value


def circle(turns):
    half = PI * turns
    square = half * half
    sine = half * series(SIN_TERMS, square)
    cosine = series(COS_TERMS, square)
    return 1.0 - 2.0 * sine * sine, 2.0 * sine * cosine


def kernel(
    sizes, spectra_far, legendre, assignment_far, circles_far, coriolis_far, weights_far,
    thickness_far, out, table, spectra, assignment, circles, coriolis, weights, thickness,
    wide, fsend, frecv, costab, sintab, coeffs, sums, bsend, brecv, proj, local, colsend, colrecv,
    load_sem, small_sem, fs_sem, fr_sem, bs_sem, br_sem, cs_sem, cr_sem,
):
    band, group, subs, stride, levels, coeff, lat, least, first_wide, last_wide, most = sizes
    pairs = 2 * levels
    widest = min(least + first_wide + last_wide, least + 1)
    block = 128 * widest
    me = lax.axis_index("band")
    mine = lax.axis_index("fld") * subs + lax.axis_index("sub")

    def width(b):
        wide_one = (b < first_wide) | (b >= band - last_wide)
        return jnp.where(wide_one, widest, least)

    def lanes(b):
        tile = b * least + jnp.minimum(b, first_wide) + jnp.maximum(b - (band - last_wide), 0)
        return pl.ds(pl.multiple_of(tile * 128, 128), block)

    def tiles(b, body):
        for c in range(widest):
            if c < least:
                body(c)
            else:
                pl.when(width(b) > c)(functools.partial(body, c))

    def tile(c):
        return pl.ds(128 * c, 128)

    def band_peer(k):
        return {"band": lax.rem(me + k, band)}

    def group_peer(k):
        peer = lax.rem(mine + k, group)
        return {"fld": peer // subs, "sub": lax.rem(peer, subs)}

    pairs_of = (
        (spectra_far, spectra), (assignment_far, assignment), (circles_far, circles),
        (coriolis_far, coriolis), (weights_far, weights), (thickness_far, thickness),
    )
    small = [
        pltpu.make_async_copy(far, near, small_sem.at[i]) for i, (far, near) in enumerate(pairs_of)
    ]
    load = pltpu.make_async_copy(legendre.at[0], table, load_sem)
    for copy in small:
        copy.start()
    load.start()
    if widest > least:
        frecv[:, :, 128 * least :] = jnp.zeros((band, 6 * pairs, 128), jnp.bfloat16)
    barrier = pltpu.get_barrier_semaphore()

    def greet_band(k):
        pl.semaphore_signal(barrier, inc=1, device_id=band_peer(k + 1), device_id_type=MESH)

    def greet_group(k):
        pl.semaphore_signal(barrier, inc=1, device_id=group_peer(k + 1), device_id_type=MESH)

    each(band - 1, greet_band)
    each(group - 1, greet_group)
    for copy in small:
        copy.wait()

    own = stride * assignment[me]
    index = lax.broadcasted_iota(jnp.int32, (2, coeff), 1)
    part = lax.broadcasted_iota(jnp.int32, (2, coeff), 0)
    keep = (index < coeff - own) & (part * jnp.where(own == 0, 1, 0) == 0)
    parity = (1 - 2 * lax.rem(index, 2)).astype(jnp.float32)
    for level in range(levels):
        for field in range(3):
            value = jnp.where(keep, spectra[0, level, field].astype(jnp.float32), 0.0)
            other = value * parity
            for r in range(2):
                row = (2 * field + r) * pairs + level
                wide[row : row + 1, :] = value[r : r + 1]
                wide[row + levels : row + levels + 1, :] = other[r : r + 1]
    both = wide[...].astype(jnp.bfloat16)

    def forward(k, c):
        return pltpu.make_async_remote_copy(
            src_ref=fsend.at[k, :, tile(c)], dst_ref=frecv.at[me, :, tile(c)],
            send_sem=fs_sem.at[k, c], recv_sem=fr_sem.at[k, c], device_id=band_peer(k + 1),
            device_id_type=MESH,
        )

    def back(k, c):
        return pltpu.make_async_remote_copy(
            src_ref=bsend.at[k, :, tile(c)], dst_ref=brecv.at[me, :, tile(c)],
            send_sem=bs_sem.at[k, c], recv_sem=br_sem.at[k, c], device_id=band_peer(k + 1),
            device_id_type=MESH,
        )

    def across(k):
        return pltpu.make_async_remote_copy(
            src_ref=colsend, dst_ref=colrecv.at[mine], send_sem=cs_sem.at[k],
            recv_sem=cr_sem.at[k], device_id=group_peer(k + 1), device_id_type=MESH,
        )

    load.wait()
    pl.semaphore_wait(barrier, band + group - 2)

    def transform(b):
        return jnp.dot(both, table[:, lanes(b)], preferred_element_type=jnp.float32).astype(
            jnp.bfloat16
        )

    def send_forward(k):
        b = lax.rem(me + k + 1, band)
        fsend[k] = transform(b)
        tiles(b, lambda c: forward(k, c).start() if c == 0 else None)

    def send_rest(wanted, k):
        b = lax.rem(me + k + 1, band)
        tiles(b, lambda c: forward(k, c).start() if c == wanted else None)

    each(band - 1, send_forward)
    for c in range(1, widest):
        each(band - 1, functools.partial(send_rest, c))
    frecv[me] = transform(me)

    for r in range(2):
        total = None
        for level in range(levels - 1, -1, -1):
            row = (4 + r) * pairs + level
            value = thickness[level] * wide[row : row + 1, :]
            total = value if total is None else total + value
            local[r, level : level + 1, :] = total
        colsend[r : r + 1, :] = total
    each(group - 1, lambda k: across(k).start())

    counts = circles[lanes(me)].astype(jnp.float32).reshape(1, block)
    ratio = jnp.floor(counts * (1.0 / stride) + 0.5)
    points = jnp.where((ratio * stride == counts) & (ratio < most), ratio, float(most))
    inverse = 1.0 / points
    height = costab.shape[2]
    xs = lax.broadcasted_iota(jnp.int32, (height, block), 0).astype(jnp.float32)
    pair = lax.broadcasted_iota(jnp.int32, (pairs, block), 0)
    lane = lax.broadcasted_iota(jnp.int32, (pairs, block), 1)
    north, south = coriolis[0:1, lanes(me)], coriolis[1:2, lanes(me)]
    spin = jnp.where(pair < levels, north, south)
    north, south = weights[0:1, lanes(me)], weights[1:2, lanes(me)]
    quad = jnp.where(pair < levels, north, south) * inverse
    quad = jnp.where(lane < 128 * width(me), quad, 0.0)

    def fill(s):
        phase = xs * assignment[s].astype(jnp.float32)
        phase = phase - points * jnp.floor(phase * inverse)
        turns = phase * inverse
        cosine, sine = circle(turns - jnp.floor(turns + 0.5))
        cosine = jnp.where(xs < points, cosine, 0.0)
        sine = jnp.where(xs < points, sine, 0.0)
        for c in range(widest):
            costab[s, c] = cosine[:, 128 * c : 128 * c + 128]
            sintab[s, c] = sine[:, 128 * c : 128 * c + 128]

    each(band, fill)

    def sample(c):
        here = slice(128 * c, 128 * c + 128)
        number = counts[:, here]

        def twice(s):
            return 2.0 * (stride * assignment[s]).astype(jnp.float32)

        def weigh(s):
            double = twice(s)
            gain = jnp.where(double < number, jnp.where(double == 0.0, 1.0, 2.0), 0.0)
            coeffs[s] = frecv[s, :, here].astype(jnp.float32) * gain

        def add_wave(x, s, fields):
            cosine = costab[s, c, pl.ds(x, 1), :]
            sine = sintab[s, c, pl.ds(x, 1), :]
            return tuple(
                fields[f]
                + coeffs[s, 2 * f * pairs : (2 * f + 1) * pairs, :] * cosine
                - coeffs[s, (2 * f + 1) * pairs : (2 * f + 2) * pairs, :] * sine
                for f in range(3)
            )

        def products(fields):
            vort, div, theta = fields
            absolute = vort + spin[:, here]
            return (
                -absolute * div,
                absolute * vort,
                0.5 * (vort * vort + div * div),
                -theta * div,
            )

        nothing = jnp.zeros((pairs, 128), jnp.float32)

        def scaled(s, q, value):
            scale = jnp.where(twice(s) < number, quad[:, here], 0.0)
            sums[s, q * pairs : (q + 1) * pairs, here] = value * scale

        each(band, weigh)
        if band <= 4:

            def point(x, totals):
                fields = (nothing,) * 3
                for s in range(band):
                    fields = add_wave(x, s, fields)
                terms = products(fields)
                result = []
                for s in range(band):
                    cosine = costab[s, c, pl.ds(x, 1), :]
                    sine = sintab[s, c, pl.ds(x, 1), :]
                    for q in range(4):
                        result.append(totals[8 * s + 2 * q] + terms[q] * cosine)
                        result.append(totals[8 * s + 2 * q + 1] - terms[q] * sine)
                return tuple(result)

            totals = lax.fori_loop(0, most, point, (nothing,) * (8 * band))
            for s in range(band):
                for q in range(8):
                    scaled(s, q, totals[8 * s + q])
        else:

            def clear(s):
                sums[s, :, here] = jnp.zeros((8 * pairs, 128), jnp.float32)

            def point(x, carry):
                fields = lax.fori_loop(
                    0, band, functools.partial(add_wave, x), (nothing,) * 3
                )
                terms = products(fields)

                def collect(s):
                    cosine = costab[s, c, pl.ds(x, 1), :]
                    sine = sintab[s, c, pl.ds(x, 1), :]
                    for q in range(4):
                        real = slice(2 * q * pairs, (2 * q + 1) * pairs)
                        imag = slice((2 * q + 1) * pairs, (2 * q + 2) * pairs)
                        sums[s, real, here] += terms[q] * cosine
                        sums[s, imag, here] -= terms[q] * sine

                each(band, collect)
                return carry

            def settle(s):
                for q in range(8):
                    scaled(s, q, sums[s, q * pairs : (q + 1) * pairs, here])

            each(band, clear)
            lax.fori_loop(0, most, point, 0)
            each(band, settle)

        def send_back(k):
            value = sums[lax.rem(me + k + 1, band), :, here]
            bsend[k, :, here] = value.astype(jnp.bfloat16)
            back(k, c).start()

        each(band - 1, send_back)
        brecv[me, :, here] = sums[me, :, here].astype(jnp.bfloat16)

    def arrive(c):
        each(band - 1, lambda k: forward(k, c).wait_recv())
        sample(c)

    tiles(me, arrive)

    def project(b, start, stop):
        lane = lanes(b)
        part = pl.ds(pl.multiple_of(lane.start + start, 128), stop - start)
        proj[...] += lax.dot_general(
            brecv[b, :, start:stop], table[:, part], (((1,), (1,)), ((), ())),
            preferred_element_type=jnp.float32,
        )

    def extra(b, body):
        pl.when(width(b) > least)(body)

    proj[...] = jnp.zeros(proj.shape, jnp.float32)
    inner = 128 * least
    if least:
        project(me, 0, inner)
    if widest > least:
        extra(me, lambda: project(me, inner, block))

    def gather_even(k):
        b = lax.rem(me + band - k - 1, band)
        for c in range(least):
            back(k, c).wait_recv()
        project(b, 0, inner)

    def gather_extra(k):
        b = lax.rem(me + band - k - 1, band)

        def last():
            back(k, least).wait_recv()
            project(b, inner, block)

        extra(b, last)

    if least:
        each(band - 1, gather_even)
    if widest > least:
        each(band - 1, gather_extra)
    each(group - 1, lambda k: across(k).wait_recv())
    below = jnp.zeros((2, coeff), jnp.float32)
    for k in range(group - 1):
        sender = lax.rem(mine + group - k - 1, group)
        below = below + jnp.where(sender > mine, 1.0, 0.0) * colrecv[sender]
    degree = own + index[0:1]
    laplace = (degree * (degree + 1)).astype(jnp.float32) * (1.0 / float((coeff - 1) * coeff))
    sign = parity[0:1]
    results = []
    for r in range(2):

        def combined(q):
            value = proj[(2 * q + r) * pairs : (2 * q + r + 1) * pairs, :]
            return value[:levels] + sign * value[levels:]

        mask = jnp.where(keep, 1.0, 0.0)[r : r + 1]
        column = local[r] + below[r : r + 1]
        second = combined(1) + laplace * (column + combined(2))
        results.append((combined(0) * mask, second * mask, combined(3) * mask))
    for level in range(levels):
        for field in range(3):
            rows = [results[r][field][level : level + 1] for r in range(2)]
            out[0, level, field] = jnp.concatenate(rows, axis=0).astype(jnp.bfloat16)

    def sent(k):
        tiles(lax.rem(me + k + 1, band), lambda c: forward(k, c).wait_send())
        tiles(me, lambda c: back(k, c).wait_send())

    each(band - 1, sent)
    each(group - 1, lambda k: across(k).wait_send())


def on_device(
    band, subs, group, spectra, legendre, assignment, circle_longitudes, coriolis, weights,
    thickness,
):
    levels, coeff, lat = spectra.shape[1], spectra.shape[4], legendre.shape[2]
    pairs = 2 * levels
    stride = coeff // band
    least, extra = divmod(lat // 128, band)
    last_wide = -(-extra // 2)
    block = 128 * (least + (1 if extra else 0))
    most = 3 * (band - 1) + 1
    height = -(-most // 8) * 8
    sizes = (
        band, group, subs, stride, levels, coeff, lat, least, extra - last_wide, last_wide, most,
    )
    far_away = pl.BlockSpec(memory_space=pltpu.MemorySpace.HBM)
    bf16, f32, dma = jnp.bfloat16, jnp.float32, pltpu.SemaphoreType.DMA
    far, near, many = max(band - 1, 1), max(group - 1, 1), block // 128
    result = pl.pallas_call(
        functools.partial(kernel, sizes),
        out_shape=jax.ShapeDtypeStruct(spectra.shape, bf16),
        in_specs=[far_away] * 7,
        out_specs=pl.BlockSpec(memory_space=pltpu.VMEM),
        scratch_shapes=[
            pltpu.VMEM((coeff, lat), bf16),
            pltpu.VMEM(spectra.shape, bf16),
            pltpu.SMEM((band,), jnp.int32),
            pltpu.VMEM((lat,), jnp.int32),
            pltpu.VMEM((2, lat), f32),
            pltpu.VMEM((2, lat), f32),
            pltpu.SMEM((levels,), f32),
            pltpu.VMEM((6 * pairs, coeff), f32),
            pltpu.VMEM((far, 6 * pairs, block), bf16),
            pltpu.VMEM((band, 6 * pairs, block), bf16),
            pltpu.VMEM((band, many, height, 128), f32),
            pltpu.VMEM((band, many, height, 128), f32),
            pltpu.VMEM((band, 6 * pairs, 128), f32),
            pltpu.VMEM((band, 8 * pairs, block), f32),
            pltpu.VMEM((far, 8 * pairs, block), bf16),
            pltpu.VMEM((band, 8 * pairs, block), bf16),
            pltpu.VMEM((8 * pairs, coeff), f32),
            pltpu.VMEM((2, levels, coeff), f32),
            pltpu.VMEM((2, coeff), f32),
            pltpu.VMEM((group, 2, coeff), f32),
            dma,
            dma((6,)),
            dma((far, many)),
            dma((far, many)),
            dma((far, many)),
            dma((far, many)),
            dma((near,)),
            dma((near,)),
        ],
        compiler_params=pltpu.CompilerParams(
            collective_id=0, has_side_effects=True, vmem_limit_bytes=64 << 20
        ),
    )(
        spectra, legendre, assignment, circle_longitudes, coriolis, weights, thickness,
    )
    return result


def solution(mesh):
    in_specs = (
        P(("member", "band"), ("fld", "sub"), None, None, None),
        P("band", None, None),
        P(),
        P(),
        P(),
        P(),
        P(("fld", "sub")),
    )
    out_specs = P(("member", "band"), ("fld", "sub"), None, None, None)
    subs = mesh.shape["sub"]
    part = functools.partial(on_device, mesh.shape["band"], subs, subs * mesh.shape["fld"])
    return jax.shard_map(
        part, mesh=mesh, in_specs=in_specs, out_specs=out_specs, check_vma=False
    )
```

```python
import functools

import jax
import jax.numpy as jnp
from jax import lax
from jax.experimental import pallas as pl
from jax.experimental.pallas import tpu as pltpu
from jax.sharding import PartitionSpec as P

MESH = pl.DeviceIdType.MESH
COS_TERMS = (1.0, -1 / 2, 1 / 24, -1 / 720, 1 / 40320, -1 / 3628800, 1 / 479001600)
SIN_TERMS = (1.0, -1 / 6, 1 / 120, -1 / 5040, 1 / 362880, -1 / 39916800, 1 / 6227020800)
PI = 3.141592653589793


def each(count, body):
    if count <= 8:
        for i in range(count):
            body(i)
    else:

        def step(i, carry):
            body(i)
            return carry

        lax.fori_loop(0, count, step, 0)


def series(terms, square):
    value = jnp.full_like(square, terms[-1])
    for term in terms[-2::-1]:
        value = value * square + term
    return value


def circle(turns):
    half = PI * turns
    square = half * half
    sine = half * series(SIN_TERMS, square)
    cosine = series(COS_TERMS, square)
    return 1.0 - 2.0 * sine * sine, 2.0 * sine * cosine


def kernel(
    sizes, spectra_far, legendre, assignment_far, circles_far, coriolis_far, weights_far,
    thickness_far, out, table, spectra, assignment, circles, coriolis, weights, thickness,
    wide, fsend, frecv, costab, sintab, coeffs, sums, bsend, brecv, proj, local, colsend, colrecv,
    load_sem, small_sem, fs_sem, fr_sem, bs_sem, br_sem, cs_sem, cr_sem,
):
    band, group, subs, stride, levels, coeff, lat, least, first_wide, last_wide, most = sizes
    pairs = 2 * levels
    widest = min(least + first_wide + last_wide, least + 1)
    block = 128 * widest
    me = lax.axis_index("band")
    mine = lax.axis_index("fld") * subs + lax.axis_index("sub")

    def width(b):
        wide_one = (b < first_wide) | (b >= band - last_wide)
        return jnp.where(wide_one, widest, least)

    def lanes(b):
        tile = b * least + jnp.minimum(b, first_wide) + jnp.maximum(b - (band - last_wide), 0)
        return pl.ds(pl.multiple_of(tile * 128, 128), block)

    def tiles(b, body):
        for c in range(widest):
            if c < least:
                body(c)
            else:
                pl.when(width(b) > c)(functools.partial(body, c))

    def tile(c):
        return pl.ds(128 * c, 128)

    def band_peer(k):
        return {"band": lax.rem(me + k, band)}

    def group_peer(k):
        peer = lax.rem(mine + k, group)
        return {"fld": peer // subs, "sub": lax.rem(peer, subs)}

    pairs_of = (
        (spectra_far, spectra), (assignment_far, assignment), (circles_far, circles),
        (coriolis_far, coriolis), (weights_far, weights), (thickness_far, thickness),
    )
    small = [
        pltpu.make_async_copy(far, near, small_sem.at[i]) for i, (far, near) in enumerate(pairs_of)
    ]
    load = pltpu.make_async_copy(legendre.at[0], table, load_sem)
    for copy in small:
        copy.start()
    load.start()
    if widest > least:
        frecv[:, :, 128 * least :] = jnp.zeros((band, 6 * pairs, 128), jnp.bfloat16)
    barrier = pltpu.get_barrier_semaphore()

    def greet_band(k):
        pl.semaphore_signal(barrier, inc=1, device_id=band_peer(k + 1), device_id_type=MESH)

    def greet_group(k):
        pl.semaphore_signal(barrier, inc=1, device_id=group_peer(k + 1), device_id_type=MESH)

    each(band - 1, greet_band)
    each(group - 1, greet_group)
    for copy in small:
        copy.wait()

    own = stride * assignment[me]
    index = lax.broadcasted_iota(jnp.int32, (2, coeff), 1)
    part = lax.broadcasted_iota(jnp.int32, (2, coeff), 0)
    keep = (index < coeff - own) & (part * jnp.where(own == 0, 1, 0) == 0)
    parity = (1 - 2 * lax.rem(index, 2)).astype(jnp.float32)
    for level in range(levels):
        for field in range(3):
            value = jnp.where(keep, spectra[0, level, field].astype(jnp.float32), 0.0)
            other = value * parity
            for r in range(2):
                row = (2 * field + r) * pairs + level
                wide[row : row + 1, :] = value[r : r + 1]
                wide[row + levels : row + levels + 1, :] = other[r : r + 1]
    both = wide[...].astype(jnp.bfloat16)

    def forward(k, c):
        return pltpu.make_async_remote_copy(
            src_ref=fsend.at[k, :, tile(c)], dst_ref=frecv.at[me, :, tile(c)],
            send_sem=fs_sem.at[k, c], recv_sem=fr_sem.at[k, c], device_id=band_peer(k + 1),
            device_id_type=MESH,
        )

    def back(k, c):
        return pltpu.make_async_remote_copy(
            src_ref=bsend.at[k, :, tile(c)], dst_ref=brecv.at[me, :, tile(c)],
            send_sem=bs_sem.at[k, c], recv_sem=br_sem.at[k, c], device_id=band_peer(k + 1),
            device_id_type=MESH,
        )

    def across(k):
        return pltpu.make_async_remote_copy(
            src_ref=colsend, dst_ref=colrecv.at[mine], send_sem=cs_sem.at[k],
            recv_sem=cr_sem.at[k], device_id=group_peer(k + 1), device_id_type=MESH,
        )

    load.wait()
    pl.semaphore_wait(barrier, band + group - 2)

    def transform(b):
        return jnp.dot(both, table[:, lanes(b)], preferred_element_type=jnp.float32).astype(
            jnp.bfloat16
        )

    def send_forward(k):
        b = lax.rem(me + k + 1, band)
        fsend[k] = transform(b)
        tiles(b, lambda c: forward(k, c).start() if c == 0 else None)

    def send_rest(wanted, k):
        b = lax.rem(me + k + 1, band)
        tiles(b, lambda c: forward(k, c).start() if c == wanted else None)

    each(band - 1, send_forward)
    for c in range(1, widest):
        each(band - 1, functools.partial(send_rest, c))
    frecv[me] = transform(me)

    for r in range(2):
        total = None
        for level in range(levels - 1, -1, -1):
            row = (4 + r) * pairs + level
            value = thickness[level] * wide[row : row + 1, :]
            total = value if total is None else total + value
            local[r, level : level + 1, :] = total
        colsend[r : r + 1, :] = total
    each(group - 1, lambda k: across(k).start())

    counts = circles[lanes(me)].astype(jnp.float32).reshape(1, block)
    ratio = jnp.floor(counts * (1.0 / stride) + 0.5)
    points = jnp.where((ratio * stride == counts) & (ratio < most), ratio, float(most))
    inverse = 1.0 / points
    height = costab.shape[2]
    xs = lax.broadcasted_iota(jnp.int32, (height, block), 0).astype(jnp.float32)
    pair = lax.broadcasted_iota(jnp.int32, (pairs, block), 0)
    lane = lax.broadcasted_iota(jnp.int32, (pairs, block), 1)
    north, south = coriolis[0:1, lanes(me)], coriolis[1:2, lanes(me)]
    spin = jnp.where(pair < levels, north, south)
    north, south = weights[0:1, lanes(me)], weights[1:2, lanes(me)]
    quad = jnp.where(pair < levels, north, south) * inverse
    quad = jnp.where(lane < 128 * width(me), quad, 0.0)

    def fill(s):
        phase = xs * assignment[s].astype(jnp.float32)
        phase = phase - points * jnp.floor(phase * inverse)
        turns = phase * inverse
        cosine, sine = circle(turns - jnp.floor(turns + 0.5))
        cosine = jnp.where(xs < points, cosine, 0.0)
        sine = jnp.where(xs < points, sine, 0.0)
        for c in range(widest):
            costab[s, c] = cosine[:, 128 * c : 128 * c + 128]
            sintab[s, c] = sine[:, 128 * c : 128 * c + 128]

    each(band, fill)

    def sample(c):
        here = slice(128 * c, 128 * c + 128)
        number = counts[:, here]

        def twice(s):
            return 2.0 * (stride * assignment[s]).astype(jnp.float32)

        def weigh(s):
            double = twice(s)
            gain = jnp.where(double < number, jnp.where(double == 0.0, 1.0, 2.0), 0.0)
            coeffs[s] = frecv[s, :, here].astype(jnp.float32) * gain

        def add_wave(x, s, fields):
            cosine = costab[s, c, pl.ds(x, 1), :]
            sine = sintab[s, c, pl.ds(x, 1), :]
            return tuple(
                fields[f]
                + coeffs[s, 2 * f * pairs : (2 * f + 1) * pairs, :] * cosine
                - coeffs[s, (2 * f + 1) * pairs : (2 * f + 2) * pairs, :] * sine
                for f in range(3)
            )

        def products(fields):
            vort, div, theta = fields
            absolute = vort + spin[:, here]
            return (
                -absolute * div,
                absolute * vort,
                0.5 * (vort * vort + div * div),
                -theta * div,
            )

        nothing = jnp.zeros((pairs, 128), jnp.float32)

        def scaled(s, q, value):
            scale = jnp.where(twice(s) < number, quad[:, here], 0.0)
            sums[s, q * pairs : (q + 1) * pairs, here] = value * scale

        each(band, weigh)
        if band <= 4:

            def point(x, totals):
                fields = (nothing,) * 3
                for s in range(band):
                    fields = add_wave(x, s, fields)
                terms = products(fields)
                result = []
                for s in range(band):
                    cosine = costab[s, c, pl.ds(x, 1), :]
                    sine = sintab[s, c, pl.ds(x, 1), :]
                    for q in range(4):
                        result.append(totals[8 * s + 2 * q] + terms[q] * cosine)
                        result.append(totals[8 * s + 2 * q + 1] - terms[q] * sine)
                return tuple(result)

            totals = (nothing,) * (8 * band)
            for x in range(most):
                totals = point(x, totals)
            for s in range(band):
                for q in range(8):
                    scaled(s, q, totals[8 * s + q])
        else:

            def clear(s):
                sums[s, :, here] = jnp.zeros((8 * pairs, 128), jnp.float32)

            def point(x, carry):
                fields = lax.fori_loop(
                    0, band, functools.partial(add_wave, x), (nothing,) * 3
                )
                terms = products(fields)

                def collect(s):
                    cosine = costab[s, c, pl.ds(x, 1), :]
                    sine = sintab[s, c, pl.ds(x, 1), :]
                    for q in range(4):
                        real = slice(2 * q * pairs, (2 * q + 1) * pairs)
                        imag = slice((2 * q + 1) * pairs, (2 * q + 2) * pairs)
                        sums[s, real, here] += terms[q] * cosine
                        sums[s, imag, here] -= terms[q] * sine

                each(band, collect)
                return carry

            def settle(s):
                for q in range(8):
                    scaled(s, q, sums[s, q * pairs : (q + 1) * pairs, here])

            each(band, clear)
            lax.fori_loop(0, most, point, 0)
            each(band, settle)

        def send_back(k):
            value = sums[lax.rem(me + k + 1, band), :, here]
            bsend[k, :, here] = value.astype(jnp.bfloat16)
            back(k, c).start()

        each(band - 1, send_back)
        brecv[me, :, here] = sums[me, :, here].astype(jnp.bfloat16)

    def arrive(c):
        each(band - 1, lambda k: forward(k, c).wait_recv())
        sample(c)

    tiles(me, arrive)

    def project(b, start, stop):
        lane = lanes(b)
        part = pl.ds(pl.multiple_of(lane.start + start, 128), stop - start)
        proj[...] += lax.dot_general(
            brecv[b, :, start:stop], table[:, part], (((1,), (1,)), ((), ())),
            preferred_element_type=jnp.float32,
        )

    def extra(b, body):
        pl.when(width(b) > least)(body)

    proj[...] = jnp.zeros(proj.shape, jnp.float32)
    inner = 128 * least
    if least:
        project(me, 0, inner)
    if widest > least:
        extra(me, lambda: project(me, inner, block))

    def gather_even(k):
        b = lax.rem(me + band - k - 1, band)
        for c in range(least):
            back(k, c).wait_recv()
        project(b, 0, inner)

    def gather_extra(k):
        b = lax.rem(me + band - k - 1, band)

        def last():
            back(k, least).wait_recv()
            project(b, inner, block)

        extra(b, last)

    if least:
        each(band - 1, gather_even)
    if widest > least:
        each(band - 1, gather_extra)
    each(group - 1, lambda k: across(k).wait_recv())
    below = jnp.zeros((2, coeff), jnp.float32)
    for k in range(group - 1):
        sender = lax.rem(mine + group - k - 1, group)
        below = below + jnp.where(sender > mine, 1.0, 0.0) * colrecv[sender]
    degree = own + index[0:1]
    laplace = (degree * (degree + 1)).astype(jnp.float32) * (1.0 / float((coeff - 1) * coeff))
    sign = parity[0:1]
    results = []
    for r in range(2):

        def combined(q):
            value = proj[(2 * q + r) * pairs : (2 * q + r + 1) * pairs, :]
            return value[:levels] + sign * value[levels:]

        mask = jnp.where(keep, 1.0, 0.0)[r : r + 1]
        column = local[r] + below[r : r + 1]
        second = combined(1) + laplace * (column + combined(2))
        results.append((combined(0) * mask, second * mask, combined(3) * mask))
    for level in range(levels):
        for field in range(3):
            rows = [results[r][field][level : level + 1] for r in range(2)]
            out[0, level, field] = jnp.concatenate(rows, axis=0)

    def sent(k):
        tiles(lax.rem(me + k + 1, band), lambda c: forward(k, c).wait_send())
        tiles(me, lambda c: back(k, c).wait_send())

    each(band - 1, sent)
    each(group - 1, lambda k: across(k).wait_send())


def on_device(
    band, subs, group, spectra, legendre, assignment, circle_longitudes, coriolis, weights,
    thickness,
):
    levels, coeff, lat = spectra.shape[1], spectra.shape[4], legendre.shape[2]
    pairs = 2 * levels
    stride = coeff // band
    least, extra = divmod(lat // 128, band)
    last_wide = -(-extra // 2)
    block = 128 * (least + (1 if extra else 0))
    most = 3 * (band - 1) + 1
    height = -(-most // 8) * 8
    sizes = (
        band, group, subs, stride, levels, coeff, lat, least, extra - last_wide, last_wide, most,
    )
    far_away = pl.BlockSpec(memory_space=pltpu.MemorySpace.HBM)
    bf16, f32, dma = jnp.bfloat16, jnp.float32, pltpu.SemaphoreType.DMA
    far, near, many = max(band - 1, 1), max(group - 1, 1), block // 128
    result = pl.pallas_call(
        functools.partial(kernel, sizes),
        out_shape=jax.ShapeDtypeStruct(spectra.shape, f32),
        in_specs=[far_away] * 7,
        out_specs=pl.BlockSpec(memory_space=pltpu.VMEM),
        scratch_shapes=[
            pltpu.VMEM((coeff, lat), bf16),
            pltpu.VMEM(spectra.shape, bf16),
            pltpu.SMEM((band,), jnp.int32),
            pltpu.VMEM((lat,), jnp.int32),
            pltpu.VMEM((2, lat), f32),
            pltpu.VMEM((2, lat), f32),
            pltpu.SMEM((levels,), f32),
            pltpu.VMEM((6 * pairs, coeff), f32),
            pltpu.VMEM((far, 6 * pairs, block), bf16),
            pltpu.VMEM((band, 6 * pairs, block), bf16),
            pltpu.VMEM((band, many, height, 128), f32),
            pltpu.VMEM((band, many, height, 128), f32),
            pltpu.VMEM((band, 6 * pairs, 128), f32),
            pltpu.VMEM((band, 8 * pairs, block), f32),
            pltpu.VMEM((far, 8 * pairs, block), bf16),
            pltpu.VMEM((band, 8 * pairs, block), bf16),
            pltpu.VMEM((8 * pairs, coeff), f32),
            pltpu.VMEM((2, levels, coeff), f32),
            pltpu.VMEM((2, coeff), f32),
            pltpu.VMEM((group, 2, coeff), f32),
            dma,
            dma((6,)),
            dma((far, many)),
            dma((far, many)),
            dma((far, many)),
            dma((far, many)),
            dma((near,)),
            dma((near,)),
        ],
        compiler_params=pltpu.CompilerParams(
            collective_id=0, has_side_effects=True, vmem_limit_bytes=64 << 20
        ),
    )(
        spectra, legendre, assignment, circle_longitudes, coriolis, weights, thickness,
    )
    return result.astype(bf16)


def solution(mesh):
    in_specs = (
        P(("member", "band"), ("fld", "sub"), None, None, None),
        P("band", None, None),
        P(),
        P(),
        P(),
        P(),
        P(("fld", "sub")),
    )
    out_specs = P(("member", "band"), ("fld", "sub"), None, None, None)
    subs = mesh.shape["sub"]
    part = functools.partial(on_device, mesh.shape["band"], subs, subs * mesh.shape["fld"])
    return jax.shard_map(
        part, mesh=mesh, in_specs=in_specs, out_specs=out_specs, check_vma=False
    )
```
